32 devices in a mesh: seq: 4 (over z), chan: 8 (over y, x, core).
Axes of the slice: x: 2, y: 2, z: 4, core: 2. Of those that a mesh axis runs over, the one named last changes fastest.
Arguments:
- q_mr: bfloat16 [2048, 8192], P('seq', 'chan'), may hold values from -6 to 6
- k_mr: bfloat16 [2048, 8192], P('seq', 'chan'), may hold values from -6 to 6
- v_mr: bfloat16 [2048, 8192], P('seq', 'chan')
- q_lr: bfloat16 [2048, 8192], P('seq', 'chan'), may hold values from -6 to 6
- k_lr: bfloat16 [2048, 8192], P('seq', 'chan'), may hold values from -6 to 6
- cotangent: bfloat16 [2048, 8192], P('seq', 'chan'), may hold values from -6 to 6
- mr_filter: bfloat16 [128, 512], P(None, 'chan'), may hold values from -0.5 to 0.5
- decay_rates: float32 [16, 512], P(None, 'chan'), as said below
- residues: float32 [16, 512], P(None, 'chan'), may hold values from -1.5 to 1.5
- norm_gain: float32 [8192], P('chan'), may hold values from 0.1 to 1.9
Outputs:
- grad_q_mr: bfloat16 [2048, 8192], P('seq', 'chan')
- grad_k_mr: bfloat16 [2048, 8192], P('seq', 'chan')
- grad_v_mr: bfloat16 [2048, 8192], P('seq', 'chan')
- grad_q_lr: bfloat16 [2048, 8192], P('seq', 'chan')
- grad_k_lr: bfloat16 [2048, 8192], P('seq', 'chan')
- grad_filter: float32 [128, 512], P(None, 'chan')
- grad_residues: float32 [16, 512], P(None, 'chan')
- grad_gain: float32 [8192], P('chan')
The draws below stay inside these ranges and needn't reach their ends.
Inputs may be any that keep to these rules, and one draw needn't show every extreme that they name: `decay_rates`: positive decay rates.
All inputs are finite; a program needn't handle non-finite values.
Results may differ from the reference program's by a relative error of at most 0.02.
Values may be sent and summed in bfloat16 or wider, within the bound.
No kernel may reach another device: no remote copies, remote signals or barrier semaphores. Data moves between devices by JAX's collectives and lax.ppermute only.
A program may use at most 192 MiB of HBM per device.

```python
import jax
import jax.numpy as jnp
from jax import lax

D = 8192
GROUP_WIDTH = 16
GROUPS = 512
MR_TAPS = 128
MODES = 16
SEQ_LEN = 2048


def draw_decay_rates(key, part):
    pick_key, slow_key, fast_key = jax.random.split(jax.random.fold_in(key, 11), 3)
    share = 0.5
    slow_pick = jax.random.uniform(pick_key, (MODES, GROUPS)) < share
    slow = jnp.exp(jax.random.uniform(slow_key, (MODES, GROUPS), minval=jnp.log(0.1 / SEQ_LEN), maxval=jnp.log(2.0 / SEQ_LEN)))
    fast = jnp.exp(jax.random.uniform(fast_key, (MODES, GROUPS), minval=jnp.log(1.0 / 50.0), maxval=jnp.log(1.0 / 30.0)))
    return jnp.where(slow_pick, slow, fast).astype(jnp.float32)


def draw_v_mr(key, part):
    base_key, row_key, col_key = jax.random.split(jax.random.fold_in(key, 23), 3)
    position = jnp.arange(D, dtype=jnp.float32) / D
    base = jax.random.truncated_normal(base_key, -4.0, 4.0, (SEQ_LEN, D))
    row_scale = jnp.exp(jnp.log(10.0) * jax.random.uniform(row_key, (SEQ_LEN,)))
    col_scale = jnp.exp(jnp.log(3.0) * position + jnp.log(10.0) * jax.random.uniform(col_key, (D,)))
    values = base * row_scale[:, None] * col_scale[None, :] / 40.0
    return values.astype(jnp.bfloat16)


def steps_of(own_key, dims, pieces, low, high):
    level = 1.0
    for dim, blocks in pieces:
        draws = jax.random.uniform(jax.random.fold_in(jax.random.fold_in(own_key, 6), dim), (blocks,), jnp.float32, low / len(pieces), high / len(pieces))
        level = level * jnp.repeat(jnp.exp(draws), dims[dim] // blocks).reshape((-1,) + (1,) * (len(dims) - 1 - dim))
    return level


def noise(rng, extent, scale, limit, cuts=(), kind=jnp.bfloat16):
    drawn = jax.random.normal(rng, extent, jnp.float32) * scale
    if len(cuts) > 0:
        drawn = steps_of(rng, extent, cuts, -0.22, 0.18) * drawn
    return jnp.clip(drawn, min=-limit, max=limit).astype(kind)


def setup_inputs(seed: int = 0) -> dict:
    splits = jax.random.split(jax.random.key(seed), 11)
    q_mr = noise(splits[0], (SEQ_LEN, D), 1.0, 6.0, ((0, 4), (1, 8)))
    k_mr = noise(splits[1], (SEQ_LEN, D), 1.0, 6.0, ((0, 4), (1, 8)))
    v_mr = draw_v_mr(jax.random.fold_in(splits[10], 71), 0)
    q_lr = noise(splits[3], (SEQ_LEN, D), 1.0, 6.0, ((0, 4), (1, 8)))
    k_lr = noise(splits[4], (SEQ_LEN, D), 1.0, 6.0, ((0, 4), (1, 8)))
    cotangent = noise(splits[5], (SEQ_LEN, D), 1.0, 6.0, ((0, 4), (1, 8)))
    mr_filter = noise(splits[6], (MR_TAPS, GROUPS), MR_TAPS ** -0.5, 0.5, ((1, 8),))
    decay_rates = draw_decay_rates(jax.random.fold_in(splits[10], 71), 0)
    residues = noise(splits[8], (MODES, GROUPS), 0.25, 1.5, ((1, 8),), jnp.float32)
    norm_gain = jnp.clip(1.0 + 0.18 * jax.random.normal(splits[9], (D,), jnp.float32), 0.1, 1.9)
    return dict(q_mr=q_mr, k_mr=k_mr, v_mr=v_mr, q_lr=q_lr, k_lr=k_lr, cotangent=cotangent, mr_filter=mr_filter, decay_rates=decay_rates, residues=residues, norm_gain=norm_gain)


EPSILON = 1e-05

def expand(params):
    return jnp.repeat(params, GROUP_WIDTH, axis=-1)

def group_sum(values):
    return lax.optimization_barrier(jnp.sum(values.reshape(values.shape[:-1] + (values.shape[-1] // GROUP_WIDTH, GROUP_WIDTH)), axis=-1))

def causal(filter_rows, signal):
    length = 2 * SEQ_LEN
    spectrum = jnp.fft.rfft(filter_rows, length, axis=0) * jnp.fft.rfft(signal, length, axis=0)
    return jnp.fft.irfft(spectrum, length, axis=0)[:SEQ_LEN]

def lagged(gradient, signal):
    length = 2 * SEQ_LEN
    spectrum = jnp.fft.rfft(gradient, length, axis=0) * jnp.conj(jnp.fft.rfft(signal, length, axis=0))
    return jnp.fft.irfft(spectrum, length, axis=0)[:SEQ_LEN]

def medium_rows(taps):
    expanded = expand(taps.astype(jnp.float32))
    return jnp.concatenate([expanded, jnp.zeros((SEQ_LEN - MR_TAPS, expanded.shape[1]), jnp.float32)], axis=0)

def long_rows(decay_rates, scaled):
    offsets = jnp.arange(SEQ_LEN, dtype=jnp.float32)[:, None]
    summed = jnp.zeros((SEQ_LEN, decay_rates.shape[1]), jnp.float32)
    for mode_index in range(MODES):
        summed = summed + scaled[mode_index][None, :] * jnp.exp(-decay_rates[mode_index][None, :] * offsets)
    return expand(summed)

def mode_sums(correlation, decay_rates):
    offsets = jnp.arange(SEQ_LEN, dtype=jnp.float32)[:, None]
    rows_out = []
    for mode_index in range(MODES):
        weights = jnp.exp(-expand(decay_rates[mode_index])[None, :] * offsets)
        rows_out.append(group_sum(lax.optimization_barrier(jnp.sum(weights * correlation, axis=0))))
    return jnp.stack(rows_out)

def reference(q_mr, k_mr, v_mr, q_lr, k_lr, cotangent, mr_filter, decay_rates, residues, norm_gain):
    stretch_cols = min(D, 512)
    block_total = D // stretch_cols
    stretch_groups = stretch_cols // GROUP_WIDTH
    block_ids = jnp.arange(block_total, dtype=jnp.int32)

    def columns_of(values, block_id):
        return lax.dynamic_slice_in_dim(values, (block_id * stretch_cols).astype(jnp.int32), stretch_cols, 1)

    def groups_of(values, block_id):
        return lax.dynamic_slice_in_dim(values, (block_id * stretch_groups).astype(jnp.int32), stretch_groups, 1)

    def rejoin(stacked):
        return jnp.moveaxis(stacked, 0, 1).reshape(stacked.shape[1], -1)
    key_value = (k_mr.astype(jnp.float32) * v_mr.astype(jnp.float32)).astype(jnp.bfloat16)
    conv_mr = rejoin(lax.map(lambda block_id: causal(medium_rows(groups_of(mr_filter, block_id)), columns_of(key_value, block_id).astype(jnp.float32)), block_ids))
    y_mr = q_mr.astype(jnp.float32) * conv_mr
    root_mean = jnp.sqrt(lax.optimization_barrier(jnp.mean(y_mr * y_mr, axis=1, keepdims=True)) + EPSILON)
    normed = y_mr / root_mean
    v_lr = (normed * norm_gain[None, :]).astype(jnp.bfloat16)
    w_lr = (k_lr.astype(jnp.float32) * v_lr.astype(jnp.float32)).astype(jnp.bfloat16)
    mode_scale = jnp.sqrt(-jnp.expm1(-2.0 * decay_rates))
    scaled = residues * mode_scale

    def long_part(block_id):
        filter_rows = long_rows(groups_of(decay_rates, block_id), groups_of(scaled, block_id))
        value_rows = columns_of(w_lr, block_id).astype(jnp.float32)
        conv_lr = causal(filter_rows, value_rows)
        grad_conv = columns_of(cotangent, block_id).astype(jnp.float32) * columns_of(q_lr, block_id).astype(jnp.float32)
        grad_w = lagged(grad_conv, filter_rows)
        mode_grad = mode_sums(lagged(grad_conv, value_rows), groups_of(decay_rates, block_id))
        return (conv_lr, grad_w, mode_grad)
    conv_parts, grad_parts, mode_parts = lax.map(long_part, block_ids)
    conv_lr = rejoin(conv_parts)
    grad_w = rejoin(grad_parts)
    mode_grad = jnp.moveaxis(mode_parts, 0, 1).reshape(MODES, GROUPS)
    grad_out = cotangent.astype(jnp.float32)
    grad_q_lr = (grad_out * conv_lr).astype(jnp.bfloat16)
    grad_k_lr = (grad_w * v_lr.astype(jnp.float32)).astype(jnp.bfloat16)
    grad_v_lr = grad_w * k_lr.astype(jnp.float32)
    grad_gain = lax.optimization_barrier(jnp.sum(grad_v_lr * normed, axis=0)) / jnp.sqrt(float(SEQ_LEN))
    grad_normed = grad_v_lr * norm_gain[None, :]
    inner_sum = lax.optimization_barrier(jnp.mean(grad_normed * normed, axis=1, keepdims=True))
    grad_y_mr = (grad_normed - normed * inner_sum) / root_mean
    grad_q_mr = (grad_y_mr * conv_mr).astype(jnp.bfloat16)
    grad_conv_mr = (grad_y_mr * q_mr.astype(jnp.float32)).astype(jnp.bfloat16)

    def medium_back(block_id):
        gradient = columns_of(grad_conv_mr, block_id).astype(jnp.float32)
        grad_kv = lagged(gradient, medium_rows(groups_of(mr_filter, block_id)))
        tap_grad = group_sum(lagged(gradient, columns_of(key_value, block_id).astype(jnp.float32))[:MR_TAPS])
        return (grad_kv, tap_grad)
    kv_parts, tap_parts = lax.map(medium_back, block_ids)
    grad_kv = rejoin(kv_parts)
    grad_filter = jnp.moveaxis(tap_parts, 0, 1).reshape(MR_TAPS, GROUPS)
    grad_k_mr = (grad_kv * v_mr.astype(jnp.float32)).astype(jnp.bfloat16)
    grad_v_mr = (grad_kv * k_mr.astype(jnp.float32)).astype(jnp.bfloat16)
    norm_terms = jnp.sqrt(float(SEQ_LEN * GROUP_WIDTH))
    return (grad_q_mr, grad_k_mr, grad_v_mr, grad_q_lr, grad_k_lr, grad_filter / norm_terms, mode_grad * mode_scale / norm_terms, grad_gain)
```

```python
import functools

import jax
import jax.numpy as jnp
from jax import lax
from jax.experimental import pallas as pl
from jax.experimental.pallas import tpu as pltpu
from jax.sharding import PartitionSpec as P

EPSILON = 1e-05
LANES = 128
F32 = jnp.float32
BF16 = jnp.bfloat16
VMEM_LIMIT = 48 * 1024 * 1024


def iota(shape, dim):
    return lax.broadcasted_iota(jnp.int32, shape, dim)


def dot(a, b):
    return jnp.dot(a, b, preferred_element_type=F32)


def dot_t(a, b, precision=None):
    return lax.dot_general(
        a, b, (((1,), (1,)), ((), ())), preferred_element_type=F32, precision=precision
    )


def scale_of(rates):
    twice = 2.0 * rates
    small = jnp.minimum(twice, 0.5)
    series = jnp.full_like(small, 1.0 / 40320.0)
    for term in (5040.0, 720.0, 120.0, 24.0, 6.0, 2.0, 1.0):
        series = 1.0 / term - small * series
    return jnp.sqrt(jnp.where(twice < 0.5, small * series, 1.0 - jnp.exp(-twice)))


def pick_column(rows, group_first, width):
    modes = rows.shape[0]
    tiled = jnp.concatenate([rows] * (LANES // width), axis=0)
    shape = tiled.shape
    chosen = iota(shape, 1) == group_first + iota(shape, 0) // modes
    return jnp.sum(jnp.where(chosen, tiled, 0.0), axis=1, keepdims=True)


def pick_groups(rows, mode, group_first, count):
    shape = (count, rows.shape[1])
    chosen = iota(shape, 1) == group_first + iota(shape, 0)
    row = jnp.broadcast_to(rows[mode : mode + 1, :], shape)
    return jnp.sum(jnp.where(chosen, row, 0.0), axis=1, keepdims=True)


def pick_channels(rows, group_first, width):
    modes = rows.shape[0]
    shape = (modes, LANES)
    total = jnp.zeros(shape, F32)
    for g in range(LANES // width):
        column = jnp.sum(
            jnp.where(iota(rows.shape, 1) == group_first + g, rows, 0.0), axis=1, keepdims=True
        )
        total = jnp.where(iota(shape, 1) // width == g, column, total)
    return total


def as_row(column):
    return jnp.transpose(jnp.broadcast_to(column, (LANES, LANES)))[0:1, :]


def fold_states(table, values, modes, width):
    full = dot(table, values)
    keep = iota(full.shape, 0) // modes == iota(full.shape, 1) // width
    full = jnp.where(keep, full, 0.0)
    total = full[0:modes]
    for g in range(1, LANES // width):
        total = total + full[g * modes : (g + 1) * modes]
    return total


def spread_states(states, width):
    modes = states.shape[0]
    tiled = jnp.concatenate([states] * (LANES // width), axis=0)
    keep = iota(tiled.shape, 0) // modes == iota(tiled.shape, 1) // width
    return jnp.where(keep, tiled, 0.0).astype(BF16)


def carry(received, rates_c, rows):
    total = received[0]
    for k in range(1, len(received)):
        total = total + jnp.exp(rates_c * (-float(rows * k))) * received[k]
    return total


def skew(row, taps):
    wide = jnp.broadcast_to(row, (taps, row.shape[1]))
    return pltpu.roll(wide, 0, 1, stride=1, stride_axis=0)


def unskew_sum(grid):
    rows, size = grid.shape
    while rows > 8:
        half = rows // 2
        grid = grid[:half] + pltpu.roll(grid[half:], size - half, 1)
        rows = half
    for bit in (1, 2, 4):
        moved = (iota(grid.shape, 0) // bit) % 2 == 1
        grid = jnp.where(moved, pltpu.roll(grid, size - bit, 1), grid)
    return jnp.sum(grid, axis=0, keepdims=True)


def keep_group(values, g, width):
    return jnp.where((iota(values.shape, 1) % LANES) // width == g, values, jnp.zeros_like(values))


def prep_kernel(width, cot, q_lr, rates_ref, res_ref, filt, states, h_out, hr_out, taps_out):
    i = pl.program_id(0)
    rows = cot.shape[0]
    taps = filt.shape[0]
    rates = rates_ref[...]
    modes = rates.shape[0]
    count = LANES // width
    first = i * count
    scaled = res_ref[...] * scale_of(rates)
    column = pick_column(rates, first, width)
    powers = jnp.exp(-column * iota((LANES, rows), 1).astype(F32)).astype(BF16)
    grad = (cot[...].astype(F32) * q_lr[...].astype(F32)).astype(BF16)
    states[...] = fold_states(powers, grad, modes, width)
    forward = iota((count, rows), 1)
    backward = rows - taps - forward
    backward = jnp.where(backward < 0, backward + rows, backward)
    forward = forward.astype(F32)
    backward = backward.astype(F32)
    h = jnp.zeros((count, rows), F32)
    hr = jnp.zeros((count, rows), F32)
    for n in range(modes):
        rate = pick_groups(rates, n, first, count)
        amount = pick_groups(scaled, n, first, count)
        h = h + amount * jnp.exp(-rate * forward)
        hr = hr + amount * jnp.exp(-rate * backward)
    h_out[...] = h
    hr_out[...] = hr

    @pl.when(i == 0)
    def _():
        lane = iota((taps, 4 * taps), 1)
        tap = iota((taps, 4 * taps), 0)
        chosen = jnp.logical_or(lane == tap, lane == 3 * taps - tap)
        select = jnp.where(chosen, 1.0, 0.0).astype(BF16)
        taps_out[...] = lax.dot_general(
            filt[...], select, (((0,), (0,)), ((), ())), preferred_element_type=F32
        )


def back_kernel(width, taps, cot, q_lr, h, out, near, far, data):
    grad = (cot[...].astype(F32) * q_lr[...].astype(F32)).astype(BF16)
    half = 2 * taps
    zero = jnp.zeros((taps, taps), BF16)
    later = iota((taps, taps), 1) >= iota((taps, taps), 0)
    for g in range(LANES // width):
        table = skew(h[g : g + 1, :], taps)
        part = [table[:, taps * d : taps * (d + 1)] for d in range(4)]
        part[0] = jnp.where(later, part[0], 0.0)
        part = [p.astype(BF16) for p in part]
        lo = g * half
        near[0:taps, lo : lo + taps] = part[0]
        near[0:taps, lo + taps : lo + half] = part[1]
        near[taps:half, lo : lo + taps] = zero
        near[taps:half, lo + taps : lo + half] = part[0]
        far[0:taps, lo : lo + taps] = part[2]
        far[0:taps, lo + taps : lo + half] = part[3]
        far[taps:half, lo : lo + taps] = part[1]
        far[taps:half, lo + taps : lo + half] = part[2]
        kept = keep_group(grad, g, width)
        data[lo : lo + half, 0:LANES] = kept[0:half]
        data[lo : lo + half, LANES : 2 * LANES] = kept[half:]
    own = dot(near[...], data[...])
    other = dot(far[...], data[:, LANES:])
    out[0:half, :] = own[:, 0:LANES] + other
    out[half:, :] = own[:, LANES:]


def medium_kernel(width, peers, *refs):
    (q, k, v, edge, taps_rows, local, k_lr, gain, rates_ref, res_ref) = refs[:10]
    received = refs[10 : 10 + peers]
    conv, grad_w, sums, table, data, acc_y, acc_n = refs[10 + peers :]
    i = pl.program_id(0)
    rows = q.shape[0]
    taps = edge.shape[0]
    blocks = rows // taps
    count = LANES // width
    first = i * count
    rates = rates_ref[...]
    scaled = res_ref[...] * scale_of(rates)
    kv = (k[...].astype(F32) * v[...].astype(F32)).astype(BF16)
    joined = jnp.concatenate([edge[...], kv], axis=0)
    for g in range(count):
        lo = g * 2 * taps
        table[:, lo : lo + 2 * taps] = skew(taps_rows[g : g + 1, :], taps).astype(BF16)
        kept = keep_group(joined, g, width)
        for b in range(blocks):
            data[lo : lo + 2 * taps, b * LANES : (b + 1) * LANES] = kept[b * taps : (b + 2) * taps]
    result = dot(table[...], data[...])
    column = pick_column(rates, first, width)
    states = carry([r[...] for r in received], pick_channels(rates, first, width), rows)
    states = states * pick_channels(scaled, first, width)
    reach = (rows - iota((rows, LANES), 0)).astype(F32)
    powers = jnp.exp(-as_row(column) * reach).astype(BF16)
    total = local[...] + dot(powers, spread_states(states, width))
    grad_w[...] = total

    @pl.when(i == 0)
    def _():
        acc_y[...] = jnp.zeros_like(acc_y)
        acc_n[...] = jnp.zeros_like(acc_n)

    for b in range(blocks):
        part = slice(b * taps, (b + 1) * taps)
        z = result[:, b * LANES : (b + 1) * LANES]
        conv[part, :] = z
        y = q[part, :].astype(F32) * z
        grad_normed = total[part, :] * k_lr[part, :].astype(F32) * gain[...]
        acc_y[part, :] += y * y
        acc_n[part, :] += grad_normed * y

    @pl.when(i == pl.num_programs(0) - 1)
    def _():
        ones = jnp.ones((8, LANES), F32)
        low = iota((8, rows), 0) < 4
        sums[...] = jnp.where(
            low,
            dot_t(ones, acc_y[...], lax.Precision.HIGHEST),
            dot_t(ones, acc_n[...], lax.Precision.HIGHEST),
        )


def norm_kernel(width, model_width, sharers, *refs):
    q, k_lr, conv, grad_w, gain, rates_ref = refs[:6]
    parts = refs[6 : 6 + sharers]
    w, grad_z, grad_edge, grad_k, grad_q, gain_part, states, inv_ref, inner_ref = refs[6 + sharers :]
    i = pl.program_id(0)
    rows = q.shape[0]
    taps = grad_edge.shape[0]
    rates = rates_ref[...]
    modes = rates.shape[0]

    @pl.when(i == 0)
    def _():
        total = parts[0][...]
        for part in parts[1:]:
            total = total + part[...]
        total = total / model_width
        inv = 1.0 / jnp.sqrt(total[0:1, :] + EPSILON)
        inner = total[7:8, :] * inv
        inv_ref[...] = jnp.transpose(jnp.broadcast_to(inv, (LANES, rows)))
        inner_ref[...] = jnp.transpose(jnp.broadcast_to(inner, (LANES, rows)))

    q_f = q[...].astype(F32)
    k_f = k_lr[...].astype(F32)
    z = conv[...]
    gw = grad_w[...]
    inv = inv_ref[...]
    normed = q_f * z * inv
    v_lr = (normed * gain[...]).astype(BF16).astype(F32)
    w_lr = (k_f * v_lr).astype(BF16)
    w[...] = w_lr
    grad_k[...] = (gw * v_lr).astype(BF16)
    grad_v = gw * k_f
    gain_part[...] = jnp.sum(grad_v * normed, axis=0, keepdims=True)
    grad_y = (grad_v * gain[...] - normed * inner_ref[...]) * inv
    grad_q[...] = (grad_y * z).astype(BF16)
    grad_conv = (grad_y * q_f).astype(BF16)
    grad_z[...] = grad_conv
    grad_edge[...] = grad_conv[0:taps]
    column = pick_column(rates, i * (LANES // width), width)
    reach = (rows - 1 - iota((LANES, rows), 1)).astype(F32)
    states[...] = fold_states(jnp.exp(-column * reach).astype(BF16), w_lr, modes, width)


def cross_kernel(
    width, grad_z, k, v, edge, cot, q_lr, w, rates_ref, gain_part, pack, left, right, wide, lags
):
    i = pl.program_id(0)
    rows = k.shape[0]
    taps = edge.shape[0]
    blocks = rows // taps
    count = LANES // width
    rates = rates_ref[...]
    modes = rates.shape[0]
    groups = rates.shape[1]
    kv = (k[...].astype(F32) * v[...].astype(F32)).astype(BF16)
    joined = jnp.concatenate([edge[...], kv], axis=0)
    gz = grad_z[...]
    side = jnp.concatenate([gz[b * taps : (b + 1) * taps] for b in range(blocks)], axis=1)
    for g in range(count):
        left[g * taps : (g + 1) * taps, :] = keep_group(side, g, width)
    for b in range(blocks):
        right[:, b * LANES : (b + 1) * LANES] = joined[b * taps : (b + 2) * taps]
    grid = dot_t(left[...], right[...])
    rows_out = [unskew_sum(grid[g * taps : (g + 1) * taps]) for g in range(count)]
    found = pltpu.roll(jnp.concatenate(rows_out, axis=0), 2 * taps - 1, 1)
    pack[pl.ds(pl.multiple_of(i * count, count), count), :] = found[:, 0:taps]
    grad = (cot[...].astype(F32) * q_lr[...].astype(F32)).astype(BF16)
    side = jnp.concatenate([grad[b * taps : (b + 1) * taps] for b in range(blocks)], axis=1)
    for g in range(count):
        left[g * taps : (g + 1) * taps, :] = keep_group(side, g, width)
    zero = jnp.zeros((taps, LANES), BF16)
    for d in range(blocks):
        at = (blocks - 1 - d) * taps
        for b in range(blocks):
            value = zero if b < d else w[(b - d) * taps : (b - d + 1) * taps, :]
            wide[at : at + taps, b * LANES : (b + 1) * LANES] = value
    lags[...] = dot_t(left[...], wide[...])
    last = rows - taps
    shape = (taps, rows)
    causal = iota(shape, 1) - last <= iota(shape, 0)
    found = [
        unskew_sum(jnp.where(causal, lags[g * taps : (g + 1) * taps, :], 0.0)) for g in range(count)
    ]
    found = jnp.concatenate(found, axis=0)
    lag = last - iota(found.shape, 1)
    lag = jnp.where(lag < 0, lag + rows, lag).astype(F32)
    result = jnp.zeros((count, LANES), F32)
    for n in range(modes):
        rate = pick_groups(rates, n, i * count, count)
        value = jnp.sum(jnp.exp(-rate * lag) * found, axis=1, keepdims=True)
        result = jnp.where(iota(result.shape, 1) == n, value, result)
    pack[pl.ds(pl.multiple_of(groups + i * count, count), count), :] = result
    pack[pl.ds(2 * groups + i, 1), :] = gain_part[...]


def join_kernel(width, rows, peers, *refs):
    pack, states, rates_ref = refs[:3]
    received = refs[3 : 3 + peers]
    out = refs[3 + peers]
    rates = rates_ref[...]
    modes, groups = rates.shape
    count = LANES // width
    out[...] = pack[...]
    for i in range(groups // count):
        part = slice(i * LANES, (i + 1) * LANES)
        rates_c = pick_channels(rates, i * count, width)
        carried = carry([r[:, part] for r in received], rates_c, rows)
        product = jnp.exp(-rates_c) * carried * states[:, part]
        shape = (LANES, LANES)
        member = jnp.where(iota((count, LANES), 1) // width == iota((count, LANES), 0), 1.0, 0.0)
        padded = jnp.concatenate([product, jnp.zeros((LANES - modes, LANES), F32)], axis=0)
        at = groups + i * count
        out[at : at + count, :] += dot_t(member, padded, lax.Precision.HIGHEST)


def last_kernel(width, peers, *refs):
    (w, cot, hr, taps_rows, grad_z, after, k, v, rates_ref, res_ref) = refs[:10]
    received = refs[10 : 10 + peers]
    grad_q, grad_k, grad_v, near, far, data, table, wide = refs[10 + peers :]
    i = pl.program_id(0)
    rows = w.shape[0]
    taps = after.shape[0]
    blocks = rows // taps
    half = 2 * taps
    count = LANES // width
    first = i * count
    rates = rates_ref[...]
    scaled = res_ref[...] * scale_of(rates)
    zero = jnp.zeros((taps, taps), BF16)
    earlier = iota((taps, taps), 1) <= iota((taps, taps), 0)
    w_lr = w[...]
    joined = jnp.concatenate([grad_z[...], after[...]], axis=0)
    for g in range(count):
        rolled = skew(hr[g : g + 1, :], taps)
        part = [rolled[:, taps * (3 - d) : taps * (4 - d)] for d in range(4)]
        part[0] = jnp.where(earlier, part[0], 0.0)
        part = [p.astype(BF16) for p in part]
        lo = g * half
        near[0:taps, lo : lo + taps] = part[0]
        near[0:taps, lo + taps : lo + half] = zero
        near[taps:half, lo : lo + taps] = part[1]
        near[taps:half, lo + taps : lo + half] = part[0]
        far[0:taps, lo : lo + taps] = part[2]
        far[0:taps, lo + taps : lo + half] = part[1]
        far[taps:half, lo : lo + taps] = part[3]
        far[taps:half, lo + taps : lo + half] = part[2]
        kept = keep_group(w_lr, g, width)
        data[lo : lo + half, 0:LANES] = kept[0:half]
        data[lo : lo + half, LANES : 2 * LANES] = kept[half:]
        table[:, lo : lo + half] = skew(taps_rows[g : g + 1, :], taps).astype(BF16)
        kept = keep_group(joined, g, width)
        for b in range(blocks):
            wide[lo : lo + half, b * LANES : (b + 1) * LANES] = kept[b * taps : (b + 2) * taps]
    own = dot(near[...], data[...])
    other = dot(far[...], data[:, 0:LANES])
    column = pick_column(rates, first, width)
    states = carry([r[...] for r in received], pick_channels(rates, first, width), rows)
    states = states * pick_channels(scaled, first, width)
    reach = (1 + iota((rows, LANES), 0)).astype(F32)
    powers = jnp.exp(-as_row(column) * reach).astype(BF16)
    outer = dot(powers, spread_states(states, width))
    grad_out = cot[...].astype(F32)
    grad_q[0:half, :] = (grad_out[0:half] * (own[:, 0:LANES] + outer[0:half])).astype(BF16)
    grad_q[half:, :] = (grad_out[half:] * (own[:, LANES:] + other + outer[half:])).astype(BF16)
    result = dot(table[...], wide[...])
    for b in range(blocks):
        part = slice(b * taps, (b + 1) * taps)
        grad_kv = result[:, b * LANES : (b + 1) * LANES]
        grad_k[part, :] = (grad_kv * v[part, :].astype(F32)).astype(BF16)
        grad_v[part, :] = (grad_kv * k[part, :].astype(F32)).astype(BF16)


def close_kernel(sharers, norm_terms, gain_terms, *refs):
    rates_ref = refs[0]
    packs = [r[...] for r in refs[1 : 1 + sharers]]
    taps_out, modes_out, gain_out = refs[1 + sharers :]
    while len(packs) > 1:
        half = len(packs) // 2
        if len(packs) % 2:
            packs = [packs[0] + packs[-1]] + packs[1:-1]
        else:
            packs = [packs[j] + packs[j + half] for j in range(half)]
    total = packs[0]
    rates = rates_ref[...]
    modes, groups = rates.shape
    taps = taps_out.shape[0]
    square = (taps, LANES)
    reverse = jnp.where(iota(square, 0) + iota(square, 1) == taps - 1, 1.0, 0.0)
    found = dot_t(reverse, total[0:groups], lax.Precision.HIGHEST)
    taps_out[...] = found * (1.0 / norm_terms)
    shape = (modes, LANES)
    same = jnp.where(iota(shape, 0) == iota(shape, 1), 1.0, 0.0)
    found = dot_t(same, total[groups : 2 * groups], lax.Precision.HIGHEST)
    modes_out[...] = found * scale_of(rates) * (1.0 / norm_terms)
    gain_out[...] = total[2 * groups :] * (1.0 / gain_terms)


def shifted(value, axis, steps):
    count = lax.axis_size(axis)
    first, last = max(0, -steps), min(count, count - steps)
    return lax.ppermute(value, axis, [(source, source + steps) for source in range(first, last)])


def rotated(value, axis, steps):
    count = lax.axis_size(axis)
    return lax.ppermute(value, axis, [(source, (source - steps) % count) for source in range(count)])


def shards(q_mr, k_mr, v_mr, q_lr, k_lr, cotangent, mr_filter, decay_rates, residues, norm_gain):
    rows, chans = q_mr.shape
    taps, groups = mr_filter.shape
    modes = decay_rates.shape[0]
    width = chans // groups
    count = LANES // width
    steps = chans // LANES
    seq_count = lax.axis_size("seq")
    chan_count = lax.axis_size("chan")
    peers = seq_count - 1
    half = 2 * taps
    gain = norm_gain.reshape(1, chans)

    wide = pl.BlockSpec((rows, LANES), lambda i: (0, i))
    edge_spec = pl.BlockSpec((taps, LANES), lambda i: (0, i))
    state_spec = pl.BlockSpec((modes, LANES), lambda i: (0, i))
    line = pl.BlockSpec((1, LANES), lambda i: (0, i))
    h_spec = pl.BlockSpec((count, rows), lambda i: (i, 0))
    down = pl.BlockSpec((count, half), lambda i: (i, 0))
    up = pl.BlockSpec((count, half), lambda i: (i, 1))

    def whole(array):
        return pl.BlockSpec(array.shape, lambda i: (0,) * len(array.shape))

    def shape(dims, dtype):
        return jax.ShapeDtypeStruct(dims, dtype)

    params = pltpu.CompilerParams(
        dimension_semantics=("arbitrary",), vmem_limit_bytes=VMEM_LIMIT
    )

    key_edge = (k_mr[rows - taps :].astype(F32) * v_mr[rows - taps :].astype(F32)).astype(BF16)
    edge = shifted(key_edge, "seq", 1)

    small = shape((modes, chans), F32)
    back_states, h, hr, taps_rows = pl.pallas_call(
        functools.partial(prep_kernel, width),
        grid=(steps,),
        in_specs=[wide, wide, whole(decay_rates), whole(residues), whole(mr_filter)],
        out_specs=[state_spec, h_spec, h_spec, pl.BlockSpec((groups, 2 * half), lambda i: (0, 0))],
        out_shape=[
            small,
            shape((groups, rows), F32),
            shape((groups, rows), F32),
            shape((groups, 2 * half), F32),
        ],
        compiler_params=params,
        name="prep",
    )(cotangent, q_lr, decay_rates, residues, mr_filter)
    from_later = [shifted(back_states, "seq", -k) for k in range(1, seq_count)]

    local = pl.pallas_call(
        functools.partial(back_kernel, width, taps),
        grid=(steps,),
        in_specs=[wide, wide, h_spec],
        out_specs=wide,
        out_shape=shape((rows, chans), F32),
        scratch_shapes=[
            pltpu.VMEM((half, count * half), BF16),
            pltpu.VMEM((half, count * half), BF16),
            pltpu.VMEM((count * half, 2 * LANES), BF16),
        ],
        compiler_params=params,
        name="back",
    )(cotangent, q_lr, h)

    conv, grad_w, sums = pl.pallas_call(
        functools.partial(medium_kernel, width, peers),
        grid=(steps,),
        in_specs=[wide, wide, wide, edge_spec, up, wide, wide, line]
        + [whole(decay_rates), whole(residues)]
        + [state_spec] * peers,
        out_specs=[wide, wide, pl.BlockSpec((8, rows), lambda i: (0, 0))],
        out_shape=[shape((rows, chans), F32), shape((rows, chans), F32), shape((8, rows), F32)],
        scratch_shapes=[
            pltpu.VMEM((taps, count * half), BF16),
            pltpu.VMEM((count * half, (rows // taps) * LANES), BF16),
            pltpu.VMEM((rows, LANES), F32),
            pltpu.VMEM((rows, LANES), F32),
        ],
        compiler_params=params,
        name="medium",
    )(q_mr, k_mr, v_mr, edge, taps_rows, local, k_lr, gain, decay_rates, residues, *from_later)

    parts = [sums] + [rotated(sums, "chan", k) for k in range(1, chan_count)]
    w, grad_z, grad_edge, grad_k_lr, grad_q_mr, gain_part, states = pl.pallas_call(
        functools.partial(norm_kernel, width, float(chans * chan_count), chan_count),
        grid=(steps,),
        in_specs=[wide, wide, wide, wide, line, whole(decay_rates)] + [whole(sums)] * chan_count,
        out_specs=[wide, wide, edge_spec, wide, wide, line, state_spec],
        out_shape=[
            shape((rows, chans), BF16),
            shape((rows, chans), BF16),
            shape((taps, chans), BF16),
            shape((rows, chans), BF16),
            shape((rows, chans), BF16),
            shape((1, chans), F32),
            small,
        ],
        scratch_shapes=[pltpu.VMEM((rows, LANES), F32), pltpu.VMEM((rows, LANES), F32)],
        compiler_params=params,
        name="norm",
    )(q_mr, k_lr, conv, grad_w, gain, decay_rates, *parts)
    from_earlier = [shifted(states, "seq", k) for k in range(1, seq_count)]
    after = shifted(grad_edge, "seq", -1)

    pack_shape = (2 * groups + steps, LANES)
    pack = pl.pallas_call(
        functools.partial(cross_kernel, width),
        grid=(steps,),
        in_specs=[wide, wide, wide, edge_spec, wide, wide, wide, whole(decay_rates), line],
        out_specs=pl.BlockSpec(pack_shape, lambda i: (0, 0)),
        out_shape=shape(pack_shape, F32),
        scratch_shapes=[
            pltpu.VMEM((count * taps, (rows // taps) * LANES), BF16),
            pltpu.VMEM((half, (rows // taps) * LANES), BF16),
            pltpu.VMEM((rows, (rows // taps) * LANES), BF16),
            pltpu.VMEM((count * taps, rows), F32),
        ],
        compiler_params=params,
        name="cross",
    )(grad_z, k_mr, v_mr, edge, cotangent, q_lr, w, decay_rates, gain_part)

    pack = pl.pallas_call(
        functools.partial(join_kernel, width, rows, peers),
        out_shape=shape(pack_shape, F32),
        compiler_params=pltpu.CompilerParams(vmem_limit_bytes=VMEM_LIMIT),
        name="join",
    )(pack, back_states, decay_rates, *from_earlier)
    packs = [pack] + [rotated(pack, "seq", k) for k in range(1, seq_count)]

    grad_q_lr, grad_k_mr, grad_v_mr = pl.pallas_call(
        functools.partial(last_kernel, width, peers),
        grid=(steps,),
        in_specs=[wide, wide, h_spec, down, wide, edge_spec, wide, wide]
        + [whole(decay_rates), whole(residues)]
        + [state_spec] * peers,
        out_specs=[wide, wide, wide],
        out_shape=[shape((rows, chans), BF16)] * 3,
        scratch_shapes=[
            pltpu.VMEM((half, count * half), BF16),
            pltpu.VMEM((half, count * half), BF16),
            pltpu.VMEM((count * half, 2 * LANES), BF16),
            pltpu.VMEM((taps, count * half), BF16),
            pltpu.VMEM((count * half, (rows // taps) * LANES), BF16),
        ],
        compiler_params=params,
        name="last",
    )(w, cotangent, hr, taps_rows, grad_z, after, k_mr, v_mr, decay_rates, residues, *from_earlier)

    total_rows = rows * seq_count
    taps_sum, mode_sum, gain_sum = pl.pallas_call(
        functools.partial(
            close_kernel, seq_count, float(total_rows * width) ** 0.5, float(total_rows) ** 0.5
        ),
        out_shape=[shape((taps, groups), F32), shape((modes, groups), F32), shape((steps, LANES), F32)],
        compiler_params=pltpu.CompilerParams(vmem_limit_bytes=VMEM_LIMIT),
        name="close",
    )(decay_rates, *packs)
    return (
        grad_q_mr,
        grad_k_mr,
        grad_v_mr,
        grad_q_lr,
        grad_k_lr,
        taps_sum,
        mode_sum,
        gain_sum.reshape(chans),
    )


def solution(mesh):
    tile = P("seq", "chan")
    column = P(None, "chan")
    return jax.shard_map(
        shards,
        mesh=mesh,
        in_specs=(tile,) * 6 + (column,) * 3 + (P("chan"),),
        out_specs=(tile,) * 5 + (column,) * 2 + (P("chan"),),
        check_vma=False,
    )
```

```python
import functools

import jax
import jax.numpy as jnp
from jax import lax
from jax.experimental import pallas as pl
from jax.experimental.pallas import tpu as pltpu
from jax.sharding import PartitionSpec as P

EPSILON = 1e-05
LANES = 128
F32 = jnp.float32
BF16 = jnp.bfloat16
VMEM_LIMIT = 24 * 1024 * 1024


def iota(shape, dim):
    return lax.broadcasted_iota(jnp.int32, shape, dim)


def dot(a, b):
    return jnp.dot(a, b, preferred_element_type=F32)


def dot_t(a, b, precision=None):
    return lax.dot_general(
        a, b, (((1,), (1,)), ((), ())), preferred_element_type=F32, precision=precision
    )


def scale_of(rates):
    twice = 2.0 * rates
    small = jnp.minimum(twice, 0.5)
    series = jnp.full_like(small, 1.0 / 40320.0)
    for term in (5040.0, 720.0, 120.0, 24.0, 6.0, 2.0, 1.0):
        series = 1.0 / term - small * series
    return jnp.sqrt(jnp.where(twice < 0.5, small * series, 1.0 - jnp.exp(-twice)))


def pick_column(rows, group_first, width):
    modes = rows.shape[0]
    tiled = jnp.concatenate([rows] * (LANES // width), axis=0)
    shape = tiled.shape
    chosen = iota(shape, 1) == group_first + iota(shape, 0) // modes
    return jnp.sum(jnp.where(chosen, tiled, 0.0), axis=1, keepdims=True)


def pick_groups(rows, mode, group_first, count):
    shape = (count, rows.shape[1])
    chosen = iota(shape, 1) == group_first + iota(shape, 0)
    row = jnp.broadcast_to(rows[mode : mode + 1, :], shape)
    return jnp.sum(jnp.where(chosen, row, 0.0), axis=1, keepdims=True)


def pick_channels(rows, group_first, width):
    modes = rows.shape[0]
    shape = (modes, LANES)
    total = jnp.zeros(shape, F32)
    for g in range(LANES // width):
        column = jnp.sum(
            jnp.where(iota(rows.shape, 1) == group_first + g, rows, 0.0), axis=1, keepdims=True
        )
        total = jnp.where(iota(shape, 1) // width == g, column, total)
    return total


def as_row(column):
    return jnp.transpose(jnp.broadcast_to(column, (LANES, LANES)))[0:1, :]


def fold_states(table, values, modes, width):
    full = dot(table, values)
    keep = iota(full.shape, 0) // modes == iota(full.shape, 1) // width
    full = jnp.where(keep, full, 0.0)
    total = full[0:modes]
    for g in range(1, LANES // width):
        total = total + full[g * modes : (g + 1) * modes]
    return total


def spread_states(states, width):
    modes = states.shape[0]
    tiled = jnp.concatenate([states] * (LANES // width), axis=0)
    keep = iota(tiled.shape, 0) // modes == iota(tiled.shape, 1) // width
    return jnp.where(keep, tiled, 0.0).astype(BF16)


def carry(received, rates_c, rows):
    total = received[0].astype(F32)
    for k in range(1, len(received)):
        total = total + jnp.exp(rates_c * (-float(rows * k))) * received[k].astype(F32)
    return total


def skew(row, taps):
    wide = jnp.broadcast_to(row, (taps, row.shape[1]))
    return pltpu.roll(wide, 0, 1, stride=1, stride_axis=0)


def unskew_sum(grid):
    rows, size = grid.shape
    while rows > 8:
        half = rows // 2
        grid = grid[:half] + pltpu.roll(grid[half:], size - half, 1)
        rows = half
    for bit in (1, 2, 4):
        moved = (iota(grid.shape, 0) // bit) % 2 == 1
        grid = jnp.where(moved, pltpu.roll(grid, size - bit, 1), grid)
    return jnp.sum(grid, axis=0, keepdims=True)


def keep_group(values, g, width):
    return jnp.where((iota(values.shape, 1) % LANES) // width == g, values, jnp.zeros_like(values))


def prep_kernel(width, cot, q_lr, rates_ref, res_ref, filt, states, h_out, hr_out, taps_out):
    i = pl.program_id(0)
    rows = cot.shape[0]
    taps = filt.shape[0]
    rates = rates_ref[...]
    modes = rates.shape[0]
    count = LANES // width
    first = i * count
    scaled = res_ref[...] * scale_of(rates)
    column = pick_column(rates, first, width)
    powers = jnp.exp(-column * iota((LANES, rows), 1).astype(F32)).astype(BF16)
    grad = (cot[...].astype(F32) * q_lr[...].astype(F32)).astype(BF16)
    states[...] = fold_states(powers, grad, modes, width).astype(BF16)
    forward = iota((count, rows), 1)
    backward = rows - taps - forward
    backward = jnp.where(backward < 0, backward + rows, backward)
    forward = forward.astype(F32)
    backward = backward.astype(F32)
    h = jnp.zeros((count, rows), F32)
    hr = jnp.zeros((count, rows), F32)
    for n in range(modes):
        rate = pick_groups(rates, n, first, count)
        amount = pick_groups(scaled, n, first, count)
        h = h + amount * jnp.exp(-rate * forward)
        hr = hr + amount * jnp.exp(-rate * backward)
    h_out[...] = h
    hr_out[...] = hr

    @pl.when(i == 0)
    def _():
        lane = iota((taps, 4 * taps), 1)
        tap = iota((taps, 4 * taps), 0)
        chosen = jnp.logical_or(lane == tap, lane == 3 * taps - tap)
        select = jnp.where(chosen, 1.0, 0.0).astype(BF16)
        taps_out[...] = lax.dot_general(
            filt[...], select, (((0,), (0,)), ((), ())), preferred_element_type=F32
        )


def back_kernel(width, taps, cot, q_lr, h, out, near, far, data):
    grad = (cot[...].astype(F32) * q_lr[...].astype(F32)).astype(BF16)
    half = 2 * taps
    zero = jnp.zeros((taps, taps), BF16)
    later = iota((taps, taps), 1) >= iota((taps, taps), 0)
    for g in range(LANES // width):
        table = skew(h[g : g + 1, :], taps)
        part = [table[:, taps * d : taps * (d + 1)] for d in range(4)]
        part[0] = jnp.where(later, part[0], 0.0)
        part = [p.astype(BF16) for p in part]
        lo = g * half
        near[0:taps, lo : lo + taps] = part[0]
        near[0:taps, lo + taps : lo + half] = part[1]
        near[taps:half, lo : lo + taps] = zero
        near[taps:half, lo + taps : lo + half] = part[0]
        far[0:taps, lo : lo + taps] = part[2]
        far[0:taps, lo + taps : lo + half] = part[3]
        far[taps:half, lo : lo + taps] = part[1]
        far[taps:half, lo + taps : lo + half] = part[2]
        kept = keep_group(grad, g, width)
        data[lo : lo + half, 0:LANES] = kept[0:half]
        data[lo : lo + half, LANES : 2 * LANES] = kept[half:]
    own = dot(near[...], data[...])
    other = dot(far[...], data[:, LANES:])
    out[0:half, :] = own[:, 0:LANES] + other
    out[half:, :] = own[:, LANES:]


def medium_kernel(width, peers, *refs):
    (q, k, v, edge, taps_rows, local, k_lr, gain, rates_ref, res_ref) = refs[:10]
    received = refs[10 : 10 + peers]
    conv, grad_w, sums, table, data, acc_y, acc_n = refs[10 + peers :]
    i = pl.program_id(0)
    rows = q.shape[0]
    taps = edge.shape[0]
    blocks = rows // taps
    count = LANES // width
    first = i * count
    rates = rates_ref[...]
    scaled = res_ref[...] * scale_of(rates)
    kv = (k[...].astype(F32) * v[...].astype(F32)).astype(BF16)
    joined = jnp.concatenate([edge[...], kv], axis=0)
    for g in range(count):
        lo = g * 2 * taps
        table[:, lo : lo + 2 * taps] = skew(taps_rows[g : g + 1, :], taps).astype(BF16)
        kept = keep_group(joined, g, width)
        for b in range(blocks):
            data[lo : lo + 2 * taps, b * LANES : (b + 1) * LANES] = kept[b * taps : (b + 2) * taps]
    result = dot(table[...], data[...])
    column = pick_column(rates, first, width)
    states = carry([r[...] for r in received], pick_channels(rates, first, width), rows)
    states = states * pick_channels(scaled, first, width)
    reach = (rows - iota((rows, LANES), 0)).astype(F32)
    powers = jnp.exp(-as_row(column) * reach).astype(BF16)
    total = local[...] + dot(powers, spread_states(states, width))
    grad_w[...] = total

    @pl.when(i == 0)
    def _():
        acc_y[...] = jnp.zeros_like(acc_y)
        acc_n[...] = jnp.zeros_like(acc_n)

    for b in range(blocks):
        part = slice(b * taps, (b + 1) * taps)
        z = result[:, b * LANES : (b + 1) * LANES]
        conv[part, :] = z
        y = q[part, :].astype(F32) * z
        grad_normed = total[part, :] * k_lr[part, :].astype(F32) * gain[...]
        acc_y[part, :] += y * y
        acc_n[part, :] += grad_normed * y

    @pl.when(i == pl.num_programs(0) - 1)
    def _():
        ones = jnp.ones((8, LANES), F32)
        low = iota((8, rows), 0) < 4
        sums[...] = jnp.where(
            low,
            dot_t(ones, acc_y[...], lax.Precision.HIGHEST),
            dot_t(ones, acc_n[...], lax.Precision.HIGHEST),
        )


def norm_kernel(width, model_width, sharers, *refs):
    q, k_lr, conv, grad_w, gain, rates_ref = refs[:6]
    parts = refs[6 : 6 + sharers]
    w, grad_z, grad_edge, grad_k, grad_q, gain_part, states, inv_ref, inner_ref = refs[6 + sharers :]
    i = pl.program_id(0)
    rows = q.shape[0]
    taps = grad_edge.shape[0]
    rates = rates_ref[...]
    modes = rates.shape[0]

    @pl.when(i == 0)
    def _():
        total = parts[0][...]
        for part in parts[1:]:
            total = total + part[...]
        total = total / model_width
        inv = 1.0 / jnp.sqrt(total[0:1, :] + EPSILON)
        inner = total[7:8, :] * inv
        inv_ref[...] = jnp.transpose(jnp.broadcast_to(inv, (LANES, rows)))
        inner_ref[...] = jnp.transpose(jnp.broadcast_to(inner, (LANES, rows)))

    q_f = q[...].astype(F32)
    k_f = k_lr[...].astype(F32)
    z = conv[...]
    gw = grad_w[...]
    inv = inv_ref[...]
    normed = q_f * z * inv
    v_lr = (normed * gain[...]).astype(BF16).astype(F32)
    w_lr = (k_f * v_lr).astype(BF16)
    w[...] = w_lr
    grad_k[...] = (gw * v_lr).astype(BF16)
    grad_v = gw * k_f
    gain_part[...] = jnp.sum(grad_v * normed, axis=0, keepdims=True)
    grad_y = (grad_v * gain[...] - normed * inner_ref[...]) * inv
    grad_q[...] = (grad_y * z).astype(BF16)
    grad_conv = (grad_y * q_f).astype(BF16)
    grad_z[...] = grad_conv
    grad_edge[...] = grad_conv[0:taps]
    column = pick_column(rates, i * (LANES // width), width)
    reach = (rows - 1 - iota((LANES, rows), 1)).astype(F32)
    found = fold_states(jnp.exp(-column * reach).astype(BF16), w_lr, modes, width)
    states[...] = found.astype(BF16)


def cross_kernel(
    width, grad_z, k, v, edge, cot, q_lr, w, rates_ref, gain_part, pack, left, right, wide, lags
):
    i = pl.program_id(0)
    rows = k.shape[0]
    taps = edge.shape[0]
    blocks = rows // taps
    count = LANES // width
    rates = rates_ref[...]
    modes = rates.shape[0]
    groups = rates.shape[1]
    kv = (k[...].astype(F32) * v[...].astype(F32)).astype(BF16)
    joined = jnp.concatenate([edge[...], kv], axis=0)
    gz = grad_z[...]
    side = jnp.concatenate([gz[b * taps : (b + 1) * taps] for b in range(blocks)], axis=1)
    for g in range(count):
        left[g * taps : (g + 1) * taps, :] = keep_group(side, g, width)
    for b in range(blocks):
        right[:, b * LANES : (b + 1) * LANES] = joined[b * taps : (b + 2) * taps]
    grid = dot_t(left[...], right[...])
    rows_out = [unskew_sum(grid[g * taps : (g + 1) * taps]) for g in range(count)]
    found = pltpu.roll(jnp.concatenate(rows_out, axis=0), 2 * taps - 1, 1)
    pack[pl.ds(pl.multiple_of(i * count, count), count), :] = found[:, 0:taps]
    grad = (cot[...].astype(F32) * q_lr[...].astype(F32)).astype(BF16)
    side = jnp.concatenate([grad[b * taps : (b + 1) * taps] for b in range(blocks)], axis=1)
    for g in range(count):
        left[g * taps : (g + 1) * taps, :] = keep_group(side, g, width)
    zero = jnp.zeros((taps, LANES), BF16)
    for d in range(blocks):
        at = (blocks - 1 - d) * taps
        for b in range(blocks):
            value = zero if b < d else w[(b - d) * taps : (b - d + 1) * taps, :]
            wide[at : at + taps, b * LANES : (b + 1) * LANES] = value
    lags[...] = dot_t(left[...], wide[...])
    last = rows - taps
    shape = (taps, rows)
    causal = iota(shape, 1) - last <= iota(shape, 0)
    found = [
        unskew_sum(jnp.where(causal, lags[g * taps : (g + 1) * taps, :], 0.0)) for g in range(count)
    ]
    found = jnp.concatenate(found, axis=0)
    lag = last - iota(found.shape, 1)
    lag = jnp.where(lag < 0, lag + rows, lag).astype(F32)
    result = jnp.zeros((count, LANES), F32)
    for n in range(modes):
        rate = pick_groups(rates, n, i * count, count)
        value = jnp.sum(jnp.exp(-rate * lag) * found, axis=1, keepdims=True)
        result = jnp.where(iota(result.shape, 1) == n, value, result)
    pack[pl.ds(pl.multiple_of(groups + i * count, count), count), :] = result
    pack[pl.ds(2 * groups + i, 1), :] = gain_part[...]


def join_kernel(width, rows, peers, *refs):
    pack, states, rates_ref = refs[:3]
    received = refs[3 : 3 + peers]
    out, total = refs[3 + peers :]
    rates = rates_ref[...]
    modes, groups = rates.shape
    count = LANES // width
    total[...] = pack[...]
    for i in range(groups // count):
        part = slice(i * LANES, (i + 1) * LANES)
        rates_c = pick_channels(rates, i * count, width)
        carried = carry([r[:, part] for r in received], rates_c, rows)
        product = jnp.exp(-rates_c) * carried * states[:, part].astype(F32)
        shape = (LANES, LANES)
        member = jnp.where(iota((count, LANES), 1) // width == iota((count, LANES), 0), 1.0, 0.0)
        padded = jnp.concatenate([product, jnp.zeros((LANES - modes, LANES), F32)], axis=0)
        at = groups + i * count
        total[at : at + count, :] += dot_t(member, padded, lax.Precision.HIGHEST)
    out[...] = total[...].astype(BF16)


def last_kernel(width, peers, *refs):
    (w, cot, hr, taps_rows, grad_z, after, k, v, rates_ref, res_ref) = refs[:10]
    received = refs[10 : 10 + peers]
    grad_q, grad_k, grad_v, mark, near, far, data, table, wide = refs[10 + peers :]
    mark[...] = jnp.zeros_like(mark)
    i = pl.program_id(0)
    rows = w.shape[0]
    taps = after.shape[0]
    blocks = rows // taps
    half = 2 * taps
    count = LANES // width
    first = i * count
    rates = rates_ref[...]
    scaled = res_ref[...] * scale_of(rates)
    zero = jnp.zeros((taps, taps), BF16)
    earlier = iota((taps, taps), 1) <= iota((taps, taps), 0)
    w_lr = w[...]
    joined = jnp.concatenate([grad_z[...], after[...]], axis=0)
    for g in range(count):
        rolled = skew(hr[g : g + 1, :], taps)
        part = [rolled[:, taps * (3 - d) : taps * (4 - d)] for d in range(4)]
        part[0] = jnp.where(earlier, part[0], 0.0)
        part = [p.astype(BF16) for p in part]
        lo = g * half
        near[0:taps, lo : lo + taps] = part[0]
        near[0:taps, lo + taps : lo + half] = zero
        near[taps:half, lo : lo + taps] = part[1]
        near[taps:half, lo + taps : lo + half] = part[0]
        far[0:taps, lo : lo + taps] = part[2]
        far[0:taps, lo + taps : lo + half] = part[1]
        far[taps:half, lo : lo + taps] = part[3]
        far[taps:half, lo + taps : lo + half] = part[2]
        kept = keep_group(w_lr, g, width)
        data[lo : lo + half, 0:LANES] = kept[0:half]
        data[lo : lo + half, LANES : 2 * LANES] = kept[half:]
        table[:, lo : lo + half] = skew(taps_rows[g : g + 1, :], taps).astype(BF16)
        kept = keep_group(joined, g, width)
        for b in range(blocks):
            wide[lo : lo + half, b * LANES : (b + 1) * LANES] = kept[b * taps : (b + 2) * taps]
    own = dot(near[...], data[...])
    other = dot(far[...], data[:, 0:LANES])
    column = pick_column(rates, first, width)
    states = carry([r[...] for r in received], pick_channels(rates, first, width), rows)
    states = states * pick_channels(scaled, first, width)
    reach = (1 + iota((rows, LANES), 0)).astype(F32)
    powers = jnp.exp(-as_row(column) * reach).astype(BF16)
    outer = dot(powers, spread_states(states, width))
    grad_out = cot[...].astype(F32)
    grad_q[0:half, :] = (grad_out[0:half] * (own[:, 0:LANES] + outer[0:half])).astype(BF16)
    grad_q[half:, :] = (grad_out[half:] * (own[:, LANES:] + other + outer[half:])).astype(BF16)
    result = dot(table[...], wide[...])
    for b in range(blocks):
        part = slice(b * taps, (b + 1) * taps)
        grad_kv = result[:, b * LANES : (b + 1) * LANES]
        grad_k[part, :] = (grad_kv * v[part, :].astype(F32)).astype(BF16)
        grad_v[part, :] = (grad_kv * k[part, :].astype(F32)).astype(BF16)


def close_kernel(sharers, norm_terms, gain_terms, *refs):
    rates_ref = refs[0]
    packs = [r[...].astype(F32) for r in refs[1 : 1 + sharers]]
    taps_out, modes_out, gain_out = refs[2 + sharers :]
    while len(packs) > 1:
        half = len(packs) // 2
        if len(packs) % 2:
            packs = [packs[0] + packs[-1]] + packs[1:-1]
        else:
            packs = [packs[j] + packs[j + half] for j in range(half)]
    total = packs[0]
    rates = rates_ref[...]
    modes, groups = rates.shape
    taps = taps_out.shape[0]
    square = (taps, LANES)
    reverse = jnp.where(iota(square, 0) + iota(square, 1) == taps - 1, 1.0, 0.0)
    found = dot_t(reverse, total[0:groups], lax.Precision.HIGHEST)
    taps_out[...] = found * (1.0 / norm_terms)
    shape = (modes, LANES)
    same = jnp.where(iota(shape, 0) == iota(shape, 1), 1.0, 0.0)
    found = dot_t(same, total[groups : 2 * groups], lax.Precision.HIGHEST)
    modes_out[...] = found * scale_of(rates) * (1.0 / norm_terms)
    gain_out[...] = total[2 * groups :] * (1.0 / gain_terms)


def shifted(value, axis, steps):
    count = lax.axis_size(axis)
    first, last = max(0, -steps), min(count, count - steps)
    return lax.ppermute(value, axis, [(source, source + steps) for source in range(first, last)])


def rotated(value, axis, steps):
    count = lax.axis_size(axis)
    return lax.ppermute(value, axis, [(source, (source - steps) % count) for source in range(count)])


def shards(q_mr, k_mr, v_mr, q_lr, k_lr, cotangent, mr_filter, decay_rates, residues, norm_gain):
    rows, chans = q_mr.shape
    taps, groups = mr_filter.shape
    modes = decay_rates.shape[0]
    width = chans // groups
    count = LANES // width
    steps = chans // LANES
    seq_count = lax.axis_size("seq")
    chan_count = lax.axis_size("chan")
    peers = seq_count - 1
    half = 2 * taps
    gain = norm_gain.reshape(1, chans)

    wide = pl.BlockSpec((rows, LANES), lambda i: (0, i))
    edge_spec = pl.BlockSpec((taps, LANES), lambda i: (0, i))
    state_spec = pl.BlockSpec((modes, LANES), lambda i: (0, i))
    line = pl.BlockSpec((1, LANES), lambda i: (0, i))
    h_spec = pl.BlockSpec((count, rows), lambda i: (i, 0))
    down = pl.BlockSpec((count, half), lambda i: (i, 0))
    up = pl.BlockSpec((count, half), lambda i: (i, 1))

    def whole(array):
        return pl.BlockSpec(array.shape, lambda i: (0,) * len(array.shape))

    def shape(dims, dtype):
        return jax.ShapeDtypeStruct(dims, dtype)

    params = pltpu.CompilerParams(
        dimension_semantics=("arbitrary",), vmem_limit_bytes=VMEM_LIMIT
    )

    key_edge = (k_mr[rows - taps :].astype(F32) * v_mr[rows - taps :].astype(F32)).astype(BF16)
    edge = shifted(key_edge, "seq", 1)
    q_mr, k_mr, v_mr, q_lr, k_lr, cotangent = [
        pltpu.with_memory_space_constraint(x, pltpu.HBM)
        for x in (q_mr, k_mr, v_mr, q_lr, k_lr, cotangent)
    ]

    small = shape((modes, chans), BF16)
    back_states, h, hr, taps_rows = pl.pallas_call(
        functools.partial(prep_kernel, width),
        grid=(steps,),
        in_specs=[wide, wide, whole(decay_rates), whole(residues), whole(mr_filter)],
        out_specs=[state_spec, h_spec, h_spec, pl.BlockSpec((groups, 2 * half), lambda i: (0, 0))],
        out_shape=[
            small,
            shape((groups, rows), F32),
            shape((groups, rows), F32),
            shape((groups, 2 * half), F32),
        ],
        compiler_params=params,
        name="prep",
    )(cotangent, q_lr, decay_rates, residues, mr_filter)
    from_later = [shifted(back_states, "seq", -k) for k in range(1, seq_count)]

    local = pl.pallas_call(
        functools.partial(back_kernel, width, taps),
        grid=(steps,),
        in_specs=[wide, wide, h_spec],
        out_specs=wide,
        out_shape=shape((rows, chans), F32),
        scratch_shapes=[
            pltpu.VMEM((half, count * half), BF16),
            pltpu.VMEM((half, count * half), BF16),
            pltpu.VMEM((count * half, 2 * LANES), BF16),
        ],
        compiler_params=params,
        name="back",
    )(cotangent, q_lr, h)

    conv, grad_w, sums = pl.pallas_call(
        functools.partial(medium_kernel, width, peers),
        grid=(steps,),
        in_specs=[wide, wide, wide, edge_spec, up, wide, wide, line]
        + [whole(decay_rates), whole(residues)]
        + [state_spec] * peers,
        out_specs=[wide, wide, pl.BlockSpec((8, rows), lambda i: (0, 0))],
        out_shape=[shape((rows, chans), F32), shape((rows, chans), F32), shape((8, rows), F32)],
        scratch_shapes=[
            pltpu.VMEM((taps, count * half), BF16),
            pltpu.VMEM((count * half, (rows // taps) * LANES), BF16),
            pltpu.VMEM((rows, LANES), F32),
            pltpu.VMEM((rows, LANES), F32),
        ],
        compiler_params=params,
        name="medium",
    )(q_mr, k_mr, v_mr, edge, taps_rows, local, k_lr, gain, decay_rates, residues, *from_later)

    parts = [sums] + [rotated(sums, "chan", k) for k in range(1, chan_count)]
    w, grad_z, grad_edge, grad_k_lr, grad_q_mr, gain_part, states = pl.pallas_call(
        functools.partial(norm_kernel, width, float(chans * chan_count), chan_count),
        grid=(steps,),
        in_specs=[wide, wide, wide, wide, line, whole(decay_rates)] + [whole(sums)] * chan_count,
        out_specs=[wide, wide, edge_spec, wide, wide, line, state_spec],
        out_shape=[
            shape((rows, chans), BF16),
            shape((rows, chans), BF16),
            shape((taps, chans), BF16),
            shape((rows, chans), BF16),
            shape((rows, chans), BF16),
            shape((1, chans), F32),
            small,
        ],
        scratch_shapes=[pltpu.VMEM((rows, LANES), F32), pltpu.VMEM((rows, LANES), F32)],
        compiler_params=params,
        name="norm",
    )(q_mr, k_lr, conv, grad_w, gain, decay_rates, *parts)
    from_earlier = [shifted(states, "seq", k) for k in range(1, seq_count)]
    after = shifted(grad_edge, "seq", -1)

    pack_shape = (2 * groups + steps, LANES)
    pack = pl.pallas_call(
        functools.partial(cross_kernel, width),
        grid=(steps,),
        in_specs=[wide, wide, wide, edge_spec, wide, wide, wide, whole(decay_rates), line],
        out_specs=pl.BlockSpec(pack_shape, lambda i: (0, 0)),
        out_shape=shape(pack_shape, F32),
        scratch_shapes=[
            pltpu.VMEM((count * taps, (rows // taps) * LANES), BF16),
            pltpu.VMEM((half, (rows // taps) * LANES), BF16),
            pltpu.VMEM((rows, (rows // taps) * LANES), BF16),
            pltpu.VMEM((count * taps, rows), F32),
        ],
        compiler_params=params,
        name="cross",
    )(grad_z, k_mr, v_mr, edge, cotangent, q_lr, w, decay_rates, gain_part)

    pack = pl.pallas_call(
        functools.partial(join_kernel, width, rows, peers),
        out_shape=shape(pack_shape, BF16),
        scratch_shapes=[pltpu.VMEM(pack_shape, F32)],
        compiler_params=pltpu.CompilerParams(vmem_limit_bytes=VMEM_LIMIT),
        name="join",
    )(pack, back_states, decay_rates, *from_earlier)
    packs = [pack] + [rotated(pack, "seq", k) for k in range(1, seq_count)]

    grad_q_lr, grad_k_mr, grad_v_mr, mark = pl.pallas_call(
        functools.partial(last_kernel, width, peers),
        grid=(steps,),
        in_specs=[wide, wide, h_spec, down, wide, edge_spec, wide, wide]
        + [whole(decay_rates), whole(residues)]
        + [state_spec] * peers,
        out_specs=[wide, wide, wide, pl.BlockSpec((8, LANES), lambda i: (0, 0))],
        out_shape=[shape((rows, chans), BF16)] * 3 + [shape((8, LANES), F32)],
        scratch_shapes=[
            pltpu.VMEM((half, count * half), BF16),
            pltpu.VMEM((half, count * half), BF16),
            pltpu.VMEM((count * half, 2 * LANES), BF16),
            pltpu.VMEM((taps, count * half), BF16),
            pltpu.VMEM((count * half, (rows // taps) * LANES), BF16),
        ],
        compiler_params=params,
        name="last",
    )(w, cotangent, hr, taps_rows, grad_z, after, k_mr, v_mr, decay_rates, residues, *from_earlier)

    in_vmem = pl.BlockSpec(memory_space=pltpu.VMEM)
    total_rows = rows * seq_count
    taps_sum, mode_sum, gain_sum = pl.pallas_call(
        functools.partial(
            close_kernel, seq_count, float(total_rows * width) ** 0.5, float(total_rows) ** 0.5
        ),
        in_specs=[in_vmem] * (1 + seq_count) + [in_vmem],
        out_shape=[shape((taps, groups), F32), shape((modes, groups), F32), shape((steps, LANES), F32)],
        compiler_params=pltpu.CompilerParams(vmem_limit_bytes=VMEM_LIMIT),
        name="close",
    )(decay_rates, *packs, mark)
    return (
        grad_q_mr,
        grad_k_mr,
        grad_v_mr,
        grad_q_lr,
        grad_k_lr,
        taps_sum,
        mode_sum,
        gain_sum.reshape(chans),
    )


def solution(mesh):
    tile = P("seq", "chan")
    column = P(None, "chan")
    return jax.shard_map(
        shards,
        mesh=mesh,
        in_specs=(tile,) * 6 + (column,) * 3 + (P("chan"),),
        out_specs=(tile,) * 5 + (column,) * 2 + (P("chan"),),
        check_vma=False,
    )
```
